32 devices in a mesh: row: 4 (over y, core), col: 4 (over z), lag: 2 (over x).
Axes of the slice: x: 2, y: 2, z: 4, core: 2. Of those that a mesh axis runs over, the one named last changes fastest.
Arguments:
- trajectories: bfloat16 [4096, 4096], P(('row', 'col'), 'lag'), may hold values from -6 to 6
- pair_live: int32 [4, 4], replicated, may hold values from 0 to 1, as said below
Outputs:
- gram: bfloat16 [4096, 4096], P(('row', 'lag'), 'col')
The draws below stay inside these ranges and needn't reach their ends.
Inputs may be any that keep to these rules, and one draw needn't show every extreme that they name: `pair_live`: Symmetric, with every diagonal entry 1.
All inputs are finite; a program needn't handle non-finite values.
Results may differ from the reference program's by a relative error of at most 0.0015.
Values may be sent and summed in bfloat16 or wider, within the bound.
A program may use at most 64 MiB of HBM per device.

```python
import math
import jax
import jax.numpy as jnp
from jax import lax

EMBED = 4096
TB = 1024
NB = 4
NT = 4096


def draw_trajectories(key, part):
    key_noise = jax.random.fold_in(key, 11)
    key_freq = jax.random.fold_in(key, 12)
    key_phase = jax.random.fold_in(key, 13)
    key_amp = jax.random.fold_in(key, 14)
    key_sigma = jax.random.fold_in(key, 15)
    noise = jnp.clip(jax.random.normal(key_noise, (NT, EMBED), jnp.float32), -4.0, 4.0)
    centre = 0.9
    spread = 0.75 * TB / EMBED
    freq = centre + spread * jax.random.uniform(key_freq, (NT,), jnp.float32, 0.0, 1.0)
    phase = jax.random.uniform(key_phase, (NT,), jnp.float32, -math.pi, math.pi)
    amp = jnp.exp(jax.random.uniform(key_amp, (NT,), jnp.float32, math.log(0.8), math.log(1.3)))
    sigma = jnp.exp(jax.random.uniform(key_sigma, (NT,), jnp.float32, math.log(0.3), math.log(0.6)))
    times = jnp.arange(EMBED, dtype=jnp.float32)
    wave = jnp.cos(freq[:, None] * times[None, :] + phase[:, None])
    values = amp[:, None] * wave + sigma[:, None] * noise
    return jnp.clip(values, -6.0, 6.0).astype(jnp.bfloat16)


def draw_pair_live(key, part):
    bits = jax.random.randint(jax.random.fold_in(key, 21), (NB, NB), 0, 2, jnp.int32)
    index = jnp.arange(NB, dtype=jnp.int32)
    upper = jnp.where(index[:, None] <= index[None, :], bits, bits.T)
    return jnp.where(index[:, None] == index[None, :], 1, upper).astype(jnp.int32)


def setup_inputs(seed: int = 0) -> dict:
    key_of = jax.random.split(jax.random.key(seed), 3)
    trajectories = draw_trajectories(jax.random.fold_in(key_of[2], 71), 0)
    pair_live = draw_pair_live(jax.random.fold_in(key_of[2], 71), 0)
    return {"trajectories": trajectories, "pair_live": pair_live}


def reference(trajectories, pair_live):
    floats = trajectories.astype(jnp.float32)
    norms = jnp.sum(floats * floats, axis=1)
    live_float = pair_live.astype(jnp.float32)

    def one_block(block_index):
        start = (block_index * TB).astype(jnp.int32)
        rows = lax.dynamic_slice_in_dim(trajectories, start, TB, 0)
        row_norm = lax.dynamic_slice_in_dim(norms, start, TB, 0)
        inner = jnp.dot(rows, trajectories.T, preferred_element_type=jnp.float32)
        dist = row_norm[:, None] + norms[None, :] - 2.0 * inner
        live_row = jnp.repeat(live_float[block_index], TB)
        return (jnp.exp(-2.0 * dist / EMBED) * live_row[None, :]).astype(jnp.bfloat16)

    blocks = lax.map(one_block, jnp.arange(NB, dtype=jnp.int32))
    return blocks.reshape(NT, NT)
```

```python
import functools

import jax
import jax.numpy as jnp
from jax import lax
from jax.experimental import pallas as pl
from jax.experimental.pallas import tpu as pltpu
from jax.sharding import PartitionSpec as P

MESH = pl.DeviceIdType.MESH
SPLIT = 2
NT_DIMS = (((1,), (1,)), ((), ()))


def kernel(
    rows, cols, lags, split, samples,
    x_ref, live_ref, out_ref,
    rb, cb, rn, cn, tile, got,
    own_sem, z_send, z_recv, c_send, c_recv, c_copy, t_send, t_recv,
):
    r, c, l = lax.axis_index("row"), lax.axis_index("col"), lax.axis_index("lag")
    units = cols * split
    m = rb.shape[1]
    mine = units // lags
    bits = rows.bit_length() - 1
    node = lax.bitwise_xor(r, c)

    own = pltpu.make_async_copy(
        x_ref, rb.at[pl.ds(c * split, split)], own_sem
    )
    own.start()

    barrier = pltpu.get_barrier_semaphore()
    for j in range(1, rows):
        pl.semaphore_signal(
            barrier, device_id={"row": lax.rem(r + j, rows)}, device_id_type=MESH
        )
    for j in range(1, lags):
        pl.semaphore_signal(
            barrier, device_id={"lag": lax.rem(l + j, lags)}, device_id_type=MESH
        )

    @pl.when(c > 0)
    def _():
        pl.semaphore_signal(barrier, device_id={"col": c - 1}, device_id_type=MESH)

    @pl.when(c < cols - 1)
    def _():
        pl.semaphore_signal(barrier, device_id={"col": c + 1}, device_id_type=MESH)

    beside = jnp.where(jnp.logical_or(c == 0, c == cols - 1), 1, 2)
    pl.semaphore_wait(barrier, rows - 1 + lags - 1 + beside)
    own.wait()

    def along(side, u):
        to = jnp.clip(c + 1 - 2 * side, 0, cols - 1)
        return pltpu.make_async_remote_copy(
            rb.at[u], rb.at[u], z_send.at[side, u], z_recv.at[u],
            device_id={"col": to}, device_id_type=MESH,
        )

    def down(bit, src, u):
        return pltpu.make_async_remote_copy(
            src.at[u], cb.at[u], c_send.at[bit, u], c_recv.at[u],
            device_id={"row": lax.bitwise_xor(r, 1 << bit)}, device_id_type=MESH,
        )

    def local(u):
        return pltpu.make_async_copy(rb.at[u], cb.at[u], c_copy.at[u])

    def has_child(bit):
        return lax.rem(node, 2 << bit) == 0

    def across(i, j):
        owner = i // mine
        hop = lax.rem(owner - l + lags, lags)
        slot = jnp.maximum(hop - 1, 0)
        return pltpu.make_async_remote_copy(
            tile.at[i, j], got.at[slot, lax.rem(i, mine), j],
            t_send.at[i, j], t_recv.at[slot, lax.rem(i, mine), j],
            device_id={"lag": owner}, device_id_type=MESH,
        )

    def valid(side, d):
        k = c - d if side == 0 else c + d
        return jnp.logical_and(k >= 0, k < cols), k

    def goes_on(side):
        return c < cols - 1 if side == 0 else c > 0

    def rank(u):
        return jnp.abs(u // split - c) * split + lax.rem(u, split)

    def one_round(q, carry):
        d, s = q // split, lax.rem(q, split)
        for side in range(2):
            ok, k = valid(side, d)
            u = jnp.clip(k, 0, cols - 1) * split + s

            @pl.when(jnp.logical_and(ok, d > 0))
            def _():
                along(side, u).wait_recv()

            @pl.when(jnp.logical_and(ok, goes_on(side)))
            def _():
                along(side, u).start()

            first = jnp.logical_and(ok, jnp.logical_or(d > 0, side == 0))

            @pl.when(jnp.logical_and(first, node == 0))
            def _():
                for bit in reversed(range(bits)):
                    down(bit, rb, u).start()
                local(u).start()

        for side in range(2):
            ok, k = valid(side, d)
            u = jnp.clip(k, 0, cols - 1) * split + s
            first = jnp.logical_and(ok, jnp.logical_or(d > 0, side == 0))

            @pl.when(first)
            def _():
                a = rb[u].astype(jnp.float32)
                rn[u] = jnp.broadcast_to(
                    jnp.sum(a * a, axis=1, keepdims=True), rn.shape[1:]
                )

            @pl.when(jnp.logical_and(first, node == 0))
            def _():
                local(u).wait()

            @pl.when(jnp.logical_and(first, node != 0))
            def _():
                down(0, cb, u).wait_recv()
                for bit in reversed(range(bits)):

                    @pl.when(has_child(bit))
                    def _():
                        down(bit, cb, u).start()

            @pl.when(first)
            def _():
                b = cb[u].astype(jnp.float32)
                n = jnp.broadcast_to(jnp.sum(b * b, axis=1, keepdims=True), (m, 128))
                cn[u] = n.T[:8]

        def one_tile(p, carry):
            i0, j = p // units, lax.rem(p, units)
            i = lax.rem(i0 + (l + 1) * mine, units)

            @pl.when(jnp.maximum(rank(i), rank(j)) == q)
            def _():
                inner = lax.dot_general(
                    rb[i], cb[j], NT_DIMS, preferred_element_type=jnp.float32
                )
                tile[i, j] = rn[i][:, :1] + cn[j][:1] - 2.0 * inner

                @pl.when(i // mine != l)
                def _():
                    across(i, j).start()

            return carry

        return lax.fori_loop(0, units * units, one_tile, carry)

    lax.fori_loop(0, units, one_round, 0)

    live = live_ref[r, c].astype(jnp.float32)

    def finish(kk, carry):
        i = l * mine + kk
        for j in range(units):
            total = tile[i, j]
            for o in range(lags - 1):
                pltpu.make_async_remote_copy(
                    tile.at[i, j], got.at[o, kk, j], t_send.at[i, j],
                    t_recv.at[o, kk, j],
                    device_id={"lag": lax.rem(l + 1, lags)}, device_id_type=MESH,
                ).wait_recv()
                total = total + got[o, kk, j]
            gram = jnp.exp(-2.0 * total / samples) * live
            out_ref[pl.ds(kk * m, m), j * m : (j + 1) * m] = gram.astype(out_ref.dtype)
        return carry

    lax.fori_loop(0, mine, finish, 0)

    def drain(u, carry):
        k = u // split

        @pl.when(jnp.logical_and(k <= c, c < cols - 1))
        def _():
            along(0, u).wait_send()

        @pl.when(jnp.logical_and(k >= c, c > 0))
        def _():
            along(1, u).wait_send()

        for bit in range(bits):

            @pl.when(has_child(bit))
            def _():
                down(bit, cb, u).wait_send()

        @pl.when(u // mine != l)
        def _():
            def each(j, carry):
                across(u, j).wait_send()
                return carry

            lax.fori_loop(0, units, each, 0)

        return carry

    lax.fori_loop(0, units, drain, 0)


def on_device(rows, cols, lags, trajectories, pair_live):
    held, width = trajectories.shape
    split = SPLIT if held % (SPLIT * 128) == 0 else 1
    m = held // split
    units = cols * split
    mine = units // lags
    bits = rows.bit_length() - 1
    dma = pltpu.SemaphoreType.DMA
    return pl.pallas_call(
        functools.partial(kernel, rows, cols, lags, split, width * lags),
        out_shape=jax.ShapeDtypeStruct((mine * m, units * m), jnp.bfloat16),
        in_specs=[
            pl.BlockSpec(memory_space=pl.ANY),
            pl.BlockSpec(memory_space=pltpu.SMEM),
        ],
        out_specs=pl.BlockSpec(memory_space=pltpu.VMEM),
        scratch_shapes=[
            pltpu.VMEM((units, m, width), jnp.bfloat16),
            pltpu.VMEM((units, m, width), jnp.bfloat16),
            pltpu.VMEM((units, m, 128), jnp.float32),
            pltpu.VMEM((units, 8, m), jnp.float32),
            pltpu.VMEM((units, units, m, m), jnp.float32),
            pltpu.VMEM((lags - 1, mine, units, m, m), jnp.float32),
            dma,
            dma((2, units)),
            dma((units,)),
            dma((bits, units)),
            dma((units,)),
            dma((units,)),
            dma((units, units)),
            dma((lags - 1, mine, units)),
        ],
        compiler_params=pltpu.CompilerParams(
            collective_id=0, has_side_effects=True, vmem_limit_bytes=60 * 2**20
        ),
    )(trajectories.reshape(split, m, width), pair_live)


def solution(mesh):
    size = mesh.shape
    return jax.shard_map(
        functools.partial(on_device, size["row"], size["col"], size["lag"]),
        mesh=mesh,
        in_specs=(P(("row", "col"), "lag"), P()),
        out_specs=P(("row", "lag"), "col"),
        check_vma=False,
    )
```

```python
import functools

import jax
import jax.numpy as jnp
from jax import lax
from jax.experimental import pallas as pl
from jax.experimental.pallas import tpu as pltpu
from jax.sharding import PartitionSpec as P

MESH = pl.DeviceIdType.MESH
SPLIT = 2
NT_DIMS = (((1,), (1,)), ((), ()))


def kernel(
    rows, cols, lags, split, samples,
    x_ref, live_ref, out_ref,
    rb, cb, rn, cn, tile, got,
    own_sem, z_send, z_recv, c_send, c_recv, c_copy, t_send, t_recv,
):
    r, c, l = lax.axis_index("row"), lax.axis_index("col"), lax.axis_index("lag")
    units = cols * split
    m = rb.shape[1]
    mine = units // lags
    bits = rows.bit_length() - 1
    node = lax.bitwise_xor(r, c)

    own = pltpu.make_async_copy(
        x_ref, rb.at[pl.ds(c * split, split)], own_sem
    )
    own.start()

    barrier = pltpu.get_barrier_semaphore()
    for j in range(1, rows):
        pl.semaphore_signal(
            barrier, device_id={"row": lax.rem(r + j, rows)}, device_id_type=MESH
        )
    for j in range(1, lags):
        pl.semaphore_signal(
            barrier, device_id={"lag": lax.rem(l + j, lags)}, device_id_type=MESH
        )

    @pl.when(c > 0)
    def _():
        pl.semaphore_signal(barrier, device_id={"col": c - 1}, device_id_type=MESH)

    @pl.when(c < cols - 1)
    def _():
        pl.semaphore_signal(barrier, device_id={"col": c + 1}, device_id_type=MESH)

    beside = jnp.where(jnp.logical_or(c == 0, c == cols - 1), 1, 2)
    pl.semaphore_wait(barrier, rows - 1 + lags - 1 + beside)
    own.wait()

    def along(side, u):
        to = jnp.clip(c + 1 - 2 * side, 0, cols - 1)
        return pltpu.make_async_remote_copy(
            rb.at[u], rb.at[u], z_send.at[side, u], z_recv.at[u],
            device_id={"col": to}, device_id_type=MESH,
        )

    def down(bit, src, u):
        return pltpu.make_async_remote_copy(
            src.at[u], cb.at[u], c_send.at[bit, u], c_recv.at[u],
            device_id={"row": lax.bitwise_xor(r, 1 << bit)}, device_id_type=MESH,
        )

    def local(u):
        return pltpu.make_async_copy(rb.at[u], cb.at[u], c_copy.at[u])

    def has_child(bit):
        return lax.rem(node, 2 << bit) == 0

    def across(i, j):
        owner = i // mine
        hop = lax.rem(owner - l + lags, lags)
        slot = jnp.maximum(hop - 1, 0)
        return pltpu.make_async_remote_copy(
            tile.at[i, j], got.at[slot, lax.rem(i, mine), j],
            t_send.at[i, j], t_recv.at[slot, lax.rem(i, mine), j],
            device_id={"lag": owner}, device_id_type=MESH,
        )

    def valid(side, d):
        k = c - d if side == 0 else c + d
        return jnp.logical_and(k >= 0, k < cols), k

    def goes_on(side):
        return c < cols - 1 if side == 0 else c > 0

    half = cols // lags
    final = (cols - 1) * split - 1

    def is_late(where, lag):
        if split == 1 or cols < 3:
            return False
        return jnp.logical_or(
            jnp.logical_and(where == 0, 1 // half == lag),
            jnp.logical_and(where == cols - 1, (cols - 2) // half == lag),
        )

    def arrival(q):
        p = q - split
        moved = jnp.where(p == final, split - 1, jnp.where(p >= split - 1, p + 1, p))
        return jnp.where(is_late(c, l), split + moved, q)

    def rank(u, lag):
        q = jnp.abs(u // split - c) * split + lax.rem(u, split)
        n = q - split
        moved = jnp.where(n == split - 1, final, jnp.where(n > split - 1, n - 1, n))
        return jnp.where(
            jnp.logical_and(is_late(c, lag), n >= 0), split + moved, q
        )

    def holds_back(side):
        if split == 1 or cols < 3:
            return False
        to = c + 1 - 2 * side
        return jnp.logical_and(to == (cols - 1 if side == 0 else 0), is_late(to, l))

    def one_round(q, carry):
        e = jnp.where(q >= split, arrival(q), q)
        d, s = e // split, lax.rem(e, split)
        for side in range(2):
            ok, k = valid(side, d)
            u = jnp.clip(k, 0, cols - 1) * split + s

            @pl.when(jnp.logical_and(ok, d > 0))
            def _():
                along(side, u).wait_recv()

            held_back = jnp.logical_and(holds_back(side), q == split - 1)

            @pl.when(
                jnp.logical_and(
                    jnp.logical_and(ok, goes_on(side)), jnp.logical_not(held_back)
                )
            )
            def _():
                along(side, u).start()

            @pl.when(jnp.logical_and(holds_back(side), q == final))
            def _():
                along(side, c * split + split - 1).start()

            first = jnp.logical_and(ok, jnp.logical_or(d > 0, side == 0))

            @pl.when(jnp.logical_and(first, node == 0))
            def _():
                for bit in reversed(range(bits)):
                    down(bit, rb, u).start()
                local(u).start()

        for side in range(2):
            ok, k = valid(side, d)
            u = jnp.clip(k, 0, cols - 1) * split + s
            first = jnp.logical_and(ok, jnp.logical_or(d > 0, side == 0))

            @pl.when(first)
            def _():
                a = rb[u].astype(jnp.float32)
                rn[u] = jnp.broadcast_to(
                    jnp.sum(a * a, axis=1, keepdims=True), rn.shape[1:]
                )

            @pl.when(jnp.logical_and(first, node == 0))
            def _():
                local(u).wait()

            @pl.when(jnp.logical_and(first, node != 0))
            def _():
                down(0, cb, u).wait_recv()
                for bit in reversed(range(bits)):

                    @pl.when(has_child(bit))
                    def _():
                        down(bit, cb, u).start()

            @pl.when(first)
            def _():
                b = cb[u].astype(jnp.float32)
                n = jnp.broadcast_to(jnp.sum(b * b, axis=1, keepdims=True), (m, 128))
                cn[u] = n.T[:8]

        def one_tile(p, carry):
            i0, j = p // units, lax.rem(p, units)
            i = lax.rem(i0 + (l + 1) * mine, units)

            @pl.when(jnp.maximum(rank(i, l), rank(j, l)) == q)
            def _():
                inner = lax.dot_general(
                    rb[i], cb[j], NT_DIMS, preferred_element_type=jnp.float32
                )
                tile[i, j] = rn[i][:, :1] + cn[j][:1] - 2.0 * inner

                @pl.when(i // mine != l)
                def _():
                    across(i, j).start()

            return carry

        return lax.fori_loop(0, units * units, one_tile, carry)

    lax.fori_loop(0, units, one_round, 0)

    live = live_ref[r, c].astype(jnp.float32)

    def finish(last, kk, carry):
        i = l * mine + kk
        for j in range(units):
            comes_last = False
            for o in range(1, lags):
                sender = lax.rem(l + o, lags)
                at = jnp.maximum(rank(i, sender), rank(j, sender))
                comes_last = jnp.logical_or(comes_last, at == units - 1)

            @pl.when(comes_last == last)
            def _():
                total = tile[i, j]
                for o in range(lags - 1):
                    pltpu.make_async_remote_copy(
                        tile.at[i, j], got.at[o, kk, j], t_send.at[i, j],
                        t_recv.at[o, kk, j],
                        device_id={"lag": lax.rem(l + 1, lags)},
                        device_id_type=MESH,
                    ).wait_recv()
                    total = total + got[o, kk, j]
                gram = jnp.exp(-2.0 * total / samples) * live
                out_ref[pl.ds(kk * m, m), j * m : (j + 1) * m] = gram.astype(
                    out_ref.dtype
                )

        return carry

    for last in (False, True):
        lax.fori_loop(0, mine, functools.partial(finish, last), 0)

    def drain(u, carry):
        k = u // split

        @pl.when(jnp.logical_and(k <= c, c < cols - 1))
        def _():
            along(0, u).wait_send()

        @pl.when(jnp.logical_and(k >= c, c > 0))
        def _():
            along(1, u).wait_send()

        for bit in range(bits):

            @pl.when(has_child(bit))
            def _():
                down(bit, cb, u).wait_send()

        @pl.when(u // mine != l)
        def _():
            def each(j, carry):
                across(u, j).wait_send()
                return carry

            lax.fori_loop(0, units, each, 0)

        return carry

    lax.fori_loop(0, units, drain, 0)


def on_device(rows, cols, lags, trajectories, pair_live):
    held, width = trajectories.shape
    split = SPLIT if held % (SPLIT * 128) == 0 else 1
    m = held // split
    units = cols * split
    mine = units // lags
    bits = rows.bit_length() - 1
    dma = pltpu.SemaphoreType.DMA
    return pl.pallas_call(
        functools.partial(kernel, rows, cols, lags, split, width * lags),
        out_shape=jax.ShapeDtypeStruct((mine * m, units * m), jnp.bfloat16),
        in_specs=[
            pl.BlockSpec(memory_space=pl.ANY),
            pl.BlockSpec(memory_space=pltpu.SMEM),
        ],
        out_specs=pl.BlockSpec(memory_space=pltpu.VMEM),
        scratch_shapes=[
            pltpu.VMEM((units, m, width), jnp.bfloat16),
            pltpu.VMEM((units, m, width), jnp.bfloat16),
            pltpu.VMEM((units, m, 128), jnp.float32),
            pltpu.VMEM((units, 8, m), jnp.float32),
            pltpu.VMEM((units, units, m, m), jnp.float32),
            pltpu.VMEM((lags - 1, mine, units, m, m), jnp.float32),
            dma,
            dma((2, units)),
            dma((units,)),
            dma((bits, units)),
            dma((units,)),
            dma((units,)),
            dma((units, units)),
            dma((lags - 1, mine, units)),
        ],
        compiler_params=pltpu.CompilerParams(
            collective_id=0, has_side_effects=True, vmem_limit_bytes=60 * 2**20
        ),
    )(trajectories.reshape(split, m, width), pair_live)


def solution(mesh):
    size = mesh.shape
    return jax.shard_map(
        functools.partial(on_device, size["row"], size["col"], size["lag"]),
        mesh=mesh,
        in_specs=(P(("row", "col"), "lag"), P()),
        out_specs=P(("row", "lag"), "col"),
        check_vma=False,
    )
```

```python
import functools

import jax
import jax.numpy as jnp
from jax import lax
from jax.experimental import pallas as pl
from jax.experimental.pallas import tpu as pltpu
from jax.sharding import PartitionSpec as P

MESH = pl.DeviceIdType.MESH
SPLIT = 2
SUB = 1
NT_DIMS = (((1,), (1,)), ((), ()))


def kernel(
    rows, cols, lags, split, samples,
    x_ref, live_ref, out_ref,
    rb, rn, cn, tile, got,
    own_sem, z_send, z_recv, c_send, c_recv, t_send, t_recv,
):
    r, c, l = lax.axis_index("row"), lax.axis_index("col"), lax.axis_index("lag")
    units = cols * split
    m = rb.shape[1]
    mine = units // lags
    bits = rows.bit_length() - 1
    node = lax.bitwise_xor(r, c)
    base = jnp.where(node == 0, 0, units)

    own = pltpu.make_async_copy(
        x_ref, rb.at[pl.ds(c * split, split)], own_sem
    )
    own.start()

    barrier = pltpu.get_barrier_semaphore()
    for j in range(1, rows):
        pl.semaphore_signal(
            barrier, device_id={"row": lax.rem(r + j, rows)}, device_id_type=MESH
        )
    for j in range(1, lags):
        pl.semaphore_signal(
            barrier, device_id={"lag": lax.rem(l + j, lags)}, device_id_type=MESH
        )

    @pl.when(c > 0)
    def _():
        pl.semaphore_signal(barrier, device_id={"col": c - 1}, device_id_type=MESH)

    @pl.when(c < cols - 1)
    def _():
        pl.semaphore_signal(barrier, device_id={"col": c + 1}, device_id_type=MESH)

    beside = jnp.where(jnp.logical_or(c == 0, c == cols - 1), 1, 2)
    pl.semaphore_wait(barrier, rows - 1 + lags - 1 + beside)
    own.wait()

    chunk = m // SUB

    def part(ref, u, h):
        return ref.at[u, pl.ds(h * chunk, chunk)]

    def along(side, u, h):
        to = jnp.clip(c + 1 - 2 * side, 0, cols - 1)
        return pltpu.make_async_remote_copy(
            part(rb, u, h), part(rb, u, h), z_send.at[side, u, h], z_recv.at[u, h],
            device_id={"col": to}, device_id_type=MESH,
        )

    def down(bit, u, h):
        return pltpu.make_async_remote_copy(
            part(rb, base + u, h), part(rb, units + u, h), c_send.at[bit, u, h], c_recv.at[u, h],
            device_id={"row": lax.bitwise_xor(r, 1 << bit)}, device_id_type=MESH,
        )

    def has_child(bit):
        return lax.rem(node, 2 << bit) == 0

    def across(i, j):
        owner = i // mine
        hop = lax.rem(owner - l + lags, lags)
        slot = jnp.maximum(hop - 1, 0)
        return pltpu.make_async_remote_copy(
            tile.at[i, j], got.at[slot, lax.rem(i, mine), j],
            t_send.at[i, j], t_recv.at[slot, lax.rem(i, mine), j],
            device_id={"lag": owner}, device_id_type=MESH,
        )

    def valid(side, d):
        k = c - d if side == 0 else c + d
        return jnp.logical_and(k >= 0, k < cols), k

    def goes_on(side):
        return c < cols - 1 if side == 0 else c > 0

    half = cols // lags
    final = (cols - 1) * split - 1

    def is_late(where, lag):
        if split == 1 or cols < 3:
            return False
        return jnp.logical_or(
            jnp.logical_and(where == 0, 1 // half == lag),
            jnp.logical_and(where == cols - 1, (cols - 2) // half == lag),
        )

    def arrival(q):
        p = q - split
        moved = jnp.where(p == final, split - 1, jnp.where(p >= split - 1, p + 1, p))
        return jnp.where(jnp.logical_and(is_late(c, l), p >= 0), split + moved, q)

    def last_unit(lag):
        far = jnp.where(2 * c < cols, cols - 1, 0)
        near = jnp.where(c == 0, 1, cols - 2)
        return jnp.where(is_late(c, lag), near, far) * split + split - 1

    def holds_back(side):
        if split == 1 or cols < 3:
            return False
        to = c + 1 - 2 * side
        return jnp.logical_and(to == (cols - 1 if side == 0 else 0), is_late(to, l))

    def unit_at(q, side):
        e = arrival(q)
        d = e // split
        ok, k = valid(side, d)
        u = jnp.clip(k, 0, cols - 1) * split + e - d * split
        return ok, jnp.logical_and(ok, jnp.logical_or(d > 0, side == 0)), u

    def one_round(q, carry):
        d = arrival(q) // split
        here = [unit_at(q, side) for side in range(2)]

        def unit(side):
            return here[side]

        def one_chunk(h, carry):
            for side in range(2):
                ok, first, u = unit(side)

                @pl.when(jnp.logical_and(ok, d > 0))
                def _():
                    along(side, u, h).wait_recv()

                held_back = jnp.logical_and(holds_back(side), q == split - 1)

                @pl.when(
                    jnp.logical_and(
                        jnp.logical_and(ok, goes_on(side)), jnp.logical_not(held_back)
                    )
                )
                def _():
                    along(side, u, h).start()

                @pl.when(jnp.logical_and(holds_back(side), q == final))
                def _():
                    along(side, c * split + split - 1, h).start()

                @pl.when(jnp.logical_and(first, node == 0))
                def _():
                    for bit in reversed(range(bits)):
                        down(bit, u, h).start()

            for side in range(2):
                ok, first, u = unit(side)

                @pl.when(jnp.logical_and(first, node != 0))
                def _():
                    down(0, u, h).wait_recv()
                    for bit in reversed(range(bits)):

                        @pl.when(has_child(bit))
                        def _():
                            down(bit, u, h).start()

            return carry

        lax.fori_loop(0, SUB, one_chunk, 0)

        for side in range(2):
            ok, first, u = unit(side)

            @pl.when(first)
            def _():
                a = rb[u].astype(jnp.float32)
                rn[u] = jnp.broadcast_to(
                    jnp.sum(a * a, axis=1, keepdims=True), rn.shape[1:]
                )
                b = rb[base + u].astype(jnp.float32)
                n = jnp.broadcast_to(jnp.sum(b * b, axis=1, keepdims=True), (m, 128))
                cn[u] = n.T[:8]

        def one_tile(i, j, leaves):
            @pl.when((i // mine != l) == leaves)
            def _():
                inner = lax.dot_general(
                    rb[i], rb[base + j], NT_DIMS, preferred_element_type=jnp.float32
                )
                tile[i, j] = rn[i][:, :1] + cn[j][:1] - 2.0 * inner
                if leaves:
                    across(i, j).start()

        def pairs(leaves, p, carry):
            q2, side2 = p // 2, lax.rem(p, 2)
            e = arrival(q2)
            d2 = e // split
            k = c + jnp.where(side2 == 0, -d2, d2)
            found = jnp.logical_and(k >= 0, k < cols)
            found = jnp.logical_and(found, jnp.logical_or(d2 > 0, side2 == 0))
            v = jnp.clip(k, 0, cols - 1) * split + e - d2 * split
            for side in range(2):
                _, first, u = unit(side)

                @pl.when(jnp.logical_and(first, found))
                def _():
                    one_tile(u, v, leaves)

                    @pl.when(q2 < q)
                    def _():
                        one_tile(v, u, leaves)

            return carry

        for leaves in (True, False):
            lax.fori_loop(0, 2 * q + 2, functools.partial(pairs, leaves), 0)
        return carry

    lax.fori_loop(0, units, one_round, 0)

    live = live_ref[r, c].astype(jnp.float32)

    def finish(last, kk, carry):
        i = l * mine + kk
        for j in range(units):
            comes_last = False
            for o in range(1, lags):
                end = last_unit(lax.rem(l + o, lags))
                comes_last = jnp.logical_or(
                    comes_last, jnp.logical_or(i == end, j == end)
                )

            @pl.when(comes_last == last)
            def _():
                total = tile[i, j]
                for o in range(lags - 1):
                    pltpu.make_async_remote_copy(
                        tile.at[i, j], got.at[o, kk, j], t_send.at[i, j],
                        t_recv.at[o, kk, j],
                        device_id={"lag": lax.rem(l + 1, lags)},
                        device_id_type=MESH,
                    ).wait_recv()
                    total = total + got[o, kk, j]
                gram = jnp.exp(-2.0 * total / samples) * live
                out_ref[pl.ds(kk * m, m), j * m : (j + 1) * m] = gram.astype(
                    out_ref.dtype
                )

        return carry

    for last in (False, True):
        lax.fori_loop(0, mine, functools.partial(finish, last), 0)

    def drain(u, carry):
        k = u // split
        for h in range(SUB):

            @pl.when(jnp.logical_and(k <= c, c < cols - 1))
            def _():
                along(0, u, h).wait_send()

            @pl.when(jnp.logical_and(k >= c, c > 0))
            def _():
                along(1, u, h).wait_send()

            for bit in range(bits):

                @pl.when(has_child(bit))
                def _():
                    down(bit, u, h).wait_send()

        @pl.when(u // mine != l)
        def _():
            def each(j, carry):
                across(u, j).wait_send()
                return carry

            lax.fori_loop(0, units, each, 0)

        return carry

    lax.fori_loop(0, units, drain, 0)


def on_device(rows, cols, lags, trajectories, pair_live):
    held, width = trajectories.shape
    split = SPLIT if held % (SPLIT * 128) == 0 else 1
    m = held // split
    units = cols * split
    mine = units // lags
    bits = rows.bit_length() - 1
    dma = pltpu.SemaphoreType.DMA
    return pl.pallas_call(
        functools.partial(kernel, rows, cols, lags, split, width * lags),
        out_shape=jax.ShapeDtypeStruct((mine * m, units * m), jnp.bfloat16),
        in_specs=[
            pl.BlockSpec(memory_space=pl.ANY),
            pl.BlockSpec(memory_space=pltpu.SMEM),
        ],
        out_specs=pl.BlockSpec(memory_space=pltpu.VMEM),
        scratch_shapes=[
            pltpu.VMEM((2 * units, m, width), jnp.bfloat16),
            pltpu.VMEM((units, m, 128), jnp.float32),
            pltpu.VMEM((units, 8, m), jnp.float32),
            pltpu.VMEM((units, units, m, m), jnp.float32),
            pltpu.VMEM((lags - 1, mine, units, m, m), jnp.float32),
            dma,
            dma((2, units, SUB)),
            dma((units, SUB)),
            dma((bits, units, SUB)),
            dma((units, SUB)),
            dma((units, units)),
            dma((lags - 1, mine, units)),
        ],
        compiler_params=pltpu.CompilerParams(
            collective_id=0, has_side_effects=True, vmem_limit_bytes=60 * 2**20
        ),
    )(trajectories.reshape(split, m, width), pair_live)


def solution(mesh):
    size = mesh.shape
    return jax.shard_map(
        functools.partial(on_device, size["row"], size["col"], size["lag"]),
        mesh=mesh,
        in_specs=(P(("row", "col"), "lag"), P()),
        out_specs=P(("row", "lag"), "col"),
        check_vma=False,
    )
```
